512 devices in a mesh: feat: 64 (over x, z, core), node: 8 (over y).
Axes of the slice: x: 4, y: 8, z: 8, core: 2. Of those that a mesh axis runs over, the one named last changes fastest.
Arguments:
- feats: bfloat16 [1024, 131072], P('feat', 'node'), may hold values from -6 to 6
- weight: bfloat16 [1024, 256], replicated, may hold values from -0.1875 to 0.1875
- tile_row: int32 [64, 8, 32], P('feat', 'node'), may hold values from 0 to 1, as said below
- tile_col: int32 [64, 8, 32], P('feat', 'node'), may hold values from 0 to 15
- tile_block: int32 [64, 8, 32], P('feat', 'node'), may hold values from 0 to 31, each once within a row
- tile_count: int32 [64, 8], P('feat', 'node'), may hold values from 8 to 32, as said below
- edge_blocks: bfloat16 [64, 8, 32, 128, 128], P('feat', 'node'), may hold values from -0.1875 to 0.1875
- cotangent: bfloat16 [256, 131072], P(None, ('node', 'feat')), may hold values from -0.016479492 to 0.016479492
Outputs:
- act: bfloat16 [256, 131072], P(None, ('node', 'feat'))
- weight_grad: float32 [1024, 256], P(('feat', 'node'))
The draws below stay inside these ranges and needn't reach their ends.
Inputs may be any that keep to these rules, and one draw needn't show every extreme that they name: Within one device block the pairs (tile_row, tile_col) of its 32 slots name every tile position once. Within one device block tile_block names each of its 32 blocks once. Slots s at or after tile_count of their block are unused; some block uses all 32 slots.
All inputs are finite; a program needn't handle non-finite values.
Results may differ from the reference program's by a relative error of at most 0.012.
Values may be sent and summed in bfloat16 or wider, within the bound.
A program may use at most 64 MiB of HBM per device.

```python
import jax
import jax.numpy as jnp
from jax import lax

FIN = 1024
HID = 256
TILE = 128
RT_DEV = 2
ROWS = 256
NODES = 131072
CLUSTER = 2048
SLOTS = 32
N_FEAT = 64
N_NODE = 8


def tile_positions(key):
    keys = jax.random.split(jax.random.fold_in(key, 17), N_FEAT * N_NODE)
    orders = jax.vmap(lambda single: jax.random.permutation(single, SLOTS))(keys)
    return orders.astype(jnp.int32).reshape(N_FEAT, N_NODE, SLOTS)


def draw_tile_row(key, part):
    return (tile_positions(key) // (N_NODE * RT_DEV)).astype(jnp.int32)


def draw_tile_col(key, part):
    return (tile_positions(key) % (N_NODE * RT_DEV)).astype(jnp.int32)


def draw_tile_count(key, part):
    levels = jax.random.randint(jax.random.fold_in(key, 5), (N_FEAT * N_NODE,), 0, 3)
    divisor = jnp.where(levels == 0, 1, jnp.where(levels == 1, 2, 4))
    counts = SLOTS // divisor
    busiest = jax.random.randint(jax.random.fold_in(key, 9), (), 0, N_FEAT * N_NODE)
    counts = counts.at[busiest].set(SLOTS)
    return counts.astype(jnp.int32).reshape(N_FEAT, N_NODE)


def shard_levels(key, dims, pieces, least, largest):
    factor_of = 1.0
    for axis_at, parts in pieces:
        draws = jax.random.uniform(jax.random.fold_in(jax.random.fold_in(key, 6), axis_at), (parts,), jnp.float32, least / len(pieces), largest / len(pieces))
        factor_of = factor_of * jnp.repeat(jnp.exp(draws), dims[axis_at] // parts).reshape((-1,) + (1,) * (len(dims) - 1 - axis_at))
    return factor_of


def scatter_about(key, shape, deviation, bound, shards=(), kind=jnp.bfloat16):
    drawn = jax.random.normal(key, shape, jnp.float32) * deviation
    if len(shards) > 0:
        drawn = shard_levels(key, shape, shards, -0.22, 0.18) * drawn
    return jnp.clip(drawn, min=-bound, max=bound).astype(kind)


def setup_inputs(seed: int = 0) -> dict:
    arg_keys = jax.random.split(jax.random.key(seed), 9)
    return {
        "feats": scatter_about(arg_keys[0], (FIN, NODES), 1.0, 6.0, ((0, 64), (1, 8))),
        "weight": scatter_about(arg_keys[1], (FIN, HID), FIN ** -0.5, 0.1875),
        "tile_row": draw_tile_row(jax.random.fold_in(arg_keys[8], 71), 0),
        "tile_col": draw_tile_col(jax.random.fold_in(arg_keys[8], 71), 0),
        "tile_block": jax.vmap(lambda own: jax.random.permutation(own, SLOTS))(jax.random.split(arg_keys[4], N_FEAT * N_NODE)).reshape((N_FEAT, N_NODE, SLOTS)).astype(jnp.int32),
        "tile_count": draw_tile_count(jax.random.fold_in(arg_keys[8], 71), 0),
        "edge_blocks": scatter_about(arg_keys[6], (N_FEAT, N_NODE, SLOTS, TILE, TILE), (TILE * RT_DEV * N_NODE // 2) ** -0.5, 0.1875, ((0, 64), (1, 8))),
        "cotangent": scatter_about(arg_keys[7], (HID, NODES), (NODES ** -0.5), 0.016479492, ((1, 512),)),
    }


root_half = 0.7071067811865476
inv_root_two_pi = 0.3989422804014327


def dense_adjacency(row_tile, col_tile, block_index, live_count, blocks, row_tiles, col_tiles):
    slot_total = row_tile.shape[0]
    tile_size = blocks.shape[-1]
    position = row_tile * col_tiles + col_tile
    places = jnp.arange(row_tiles * col_tiles, dtype=jnp.int32)
    active = jnp.arange(slot_total, dtype=jnp.int32) < live_count
    matches = (position[None, :] == places[:, None]) & active[None, :]
    chosen = jnp.sum(jnp.where(matches, block_index[None, :], 0), axis=1).astype(jnp.int32)
    filled = jnp.any(matches, axis=1)
    picked = jnp.take(blocks, chosen, axis=0) * filled[:, None, None].astype(blocks.dtype)
    layout = picked.reshape(row_tiles, col_tiles, tile_size, tile_size)
    return layout.transpose(0, 2, 1, 3).reshape(row_tiles * tile_size, col_tiles * tile_size)


def gelu_parts(preact):
    normal_cdf = 0.5 * (1.0 + lax.erf(preact * root_half))
    normal_pdf = jnp.exp(-0.5 * preact * preact) * inv_root_two_pi
    return preact * normal_cdf, normal_cdf + preact * normal_pdf


def reference(feats, weight, tile_row, tile_col, tile_block, tile_count, edge_blocks, cotangent):
    projected = jnp.dot(weight.T, feats, preferred_element_type=jnp.float32)
    proj_four = projected.reshape(HID, N_NODE, N_FEAT, ROWS)
    cot_four = cotangent.reshape(HID, N_NODE, N_FEAT, ROWS)

    def per_cluster(fidx):
        cluster_proj = proj_four[:, :, fidx, :].reshape(HID, CLUSTER)

        def per_block(nidx):
            adjacency = dense_adjacency(tile_row[fidx, nidx], tile_col[fidx, nidx], tile_block[fidx, nidx],
                                        tile_count[fidx, nidx], edge_blocks[fidx, nidx], RT_DEV,
                                        N_NODE * RT_DEV).astype(jnp.float32)
            preact = jnp.dot(cluster_proj, adjacency.T, precision=lax.Precision.HIGHEST)
            output, derivative = gelu_parts(preact)
            pre_grad = cot_four[:, nidx, fidx, :].astype(jnp.float32) * derivative
            node_terms = jnp.dot(adjacency.T, pre_grad.T, precision=lax.Precision.HIGHEST)
            return output.astype(jnp.bfloat16), node_terms

        outputs, node_terms = lax.map(per_block, jnp.arange(N_NODE, dtype=jnp.int32))
        return outputs, jnp.sum(node_terms, axis=0)

    outputs, node_sums = lax.map(per_cluster, jnp.arange(N_FEAT, dtype=jnp.int32))
    act = outputs.transpose(2, 1, 0, 3).reshape(HID, NODES)
    node_grad = node_sums.reshape(N_FEAT, N_NODE, ROWS, HID).transpose(1, 0, 2, 3).reshape(NODES, HID)
    weight_grad = jnp.dot(feats.astype(jnp.float32), node_grad, precision=lax.Precision.HIGHEST)
    return act, weight_grad
```

```python
import jax
import jax.numpy as jnp
from jax import lax
from jax.sharding import PartitionSpec as P

root_half = 0.7071067811865476
inv_root_two_pi = 0.3989422804014327


def dense_adjacency(row_tile, col_tile, block_index, live_count, blocks, row_tiles, col_tiles):
    slot_total = row_tile.shape[0]
    tile_size = blocks.shape[-1]
    position = row_tile * col_tiles + col_tile
    places = jnp.arange(row_tiles * col_tiles, dtype=jnp.int32)
    active = jnp.arange(slot_total, dtype=jnp.int32) < live_count
    matches = (position[None, :] == places[:, None]) & active[None, :]
    chosen = jnp.sum(jnp.where(matches, block_index[None, :], 0), axis=1)
    filled = jnp.any(matches, axis=1)
    picked = jnp.take(blocks, chosen, axis=0) * filled[:, None, None].astype(blocks.dtype)
    layout = picked.reshape(row_tiles, col_tiles, tile_size, tile_size)
    return layout.transpose(0, 2, 1, 3).reshape(row_tiles * tile_size, col_tiles * tile_size)


def gelu_parts(preact):
    normal_cdf = 0.5 * (1.0 + lax.erf(preact * root_half))
    normal_pdf = jnp.exp(-0.5 * preact * preact) * inv_root_two_pi
    return (preact * normal_cdf, normal_cdf + preact * normal_pdf)


def two_part(values):
    upper = lax.optimization_barrier(values.astype(jnp.bfloat16))
    lower = (values - upper.astype(jnp.float32)).astype(jnp.bfloat16)
    return (upper, lower)


def split_dot(left, right, dims):
    left_hi, left_lo = two_part(left)
    total = lax.dot_general(left_hi, right, dims, preferred_element_type=jnp.float32)
    return total + lax.dot_general(left_lo, right, dims, preferred_element_type=jnp.float32)


def per_device(feats, weight, tile_row, tile_col, tile_block, tile_count, edge_blocks, cotangent):
    feat_devices = lax.axis_size("feat")
    part_width, shard_nodes = feats.shape
    own_rows = shard_nodes // feat_devices
    tile_size = edge_blocks.shape[-1]
    row_tiles = own_rows // tile_size
    slot_total = edge_blocks.shape[2]
    adjacency = dense_adjacency(
        tile_row[0, 0],
        tile_col[0, 0],
        tile_block[0, 0],
        tile_count[0, 0],
        edge_blocks[0, 0],
        row_tiles,
        slot_total // row_tiles,
    )
    by_dest = feats.reshape(part_width, feat_devices, own_rows)
    contract_last = (((1,), (1,)), ((), ()))
    contract_first = (((0,), (0,)), ((), ()))
    arrive_local_rows = lax.all_to_all(by_dest, "feat", split_axis=1, concat_axis=0, tiled=True)[
        :, 0, :
    ]
    projected = lax.dot_general(
        weight, arrive_local_rows, contract_first, preferred_element_type=jnp.float32
    )
    local_rows, projected = (arrive_local_rows, projected)
    columns = adjacency
    gathered = lax.all_gather(projected.astype(jnp.bfloat16), "node", axis=1, tiled=True)
    preact = lax.dot_general(gathered, columns, contract_last, preferred_element_type=jnp.float32)
    output, derivative = gelu_parts(preact)
    pre_grad = cotangent.astype(jnp.float32) * derivative
    grad_hi, grad_lo = two_part(pre_grad)
    columns = adjacency
    total = lax.dot_general(
        columns, grad_hi, (((0,), (1,)), ((), ())), preferred_element_type=jnp.float32
    )
    node_grad = lax.psum_scatter(
        (
            total
            + lax.dot_general(
                columns, grad_lo, (((0,), (1,)), ((), ())), preferred_element_type=jnp.float32
            )
        ).astype(jnp.bfloat16),
        "node",
        scatter_dimension=0,
        tiled=True,
    ).astype(jnp.float32)
    node_hi, node_lo = two_part(node_grad)
    total = jnp.dot(local_rows, node_hi, preferred_element_type=jnp.float32)
    total = total + jnp.dot(local_rows, node_lo, preferred_element_type=jnp.float32)
    terms = total.astype(jnp.bfloat16).reshape(feat_devices, part_width, -1)
    terms = lax.all_to_all(terms, "feat", split_axis=0, concat_axis=0, tiled=True)
    feat_sum = jnp.sum(terms.astype(jnp.float32), axis=0)
    node_devices = lax.axis_size("node")
    shares = feat_sum.reshape(node_devices, part_width // node_devices, -1)
    shares = lax.all_to_all(shares, "node", split_axis=0, concat_axis=0, tiled=True)
    weight_grad = jnp.sum(shares, axis=0)
    return (output.astype(jnp.bfloat16), weight_grad)


def solution(mesh):
    return jax.shard_map(
        per_device,
        mesh=mesh,
        in_specs=(
            P("feat", "node"),
            P(),
            P("feat", "node", None),
            P("feat", "node", None),
            P("feat", "node", None),
            P("feat", "node"),
            P("feat", "node", None, None, None),
            P(None, ("node", "feat")),
        ),
        out_specs=(P(None, ("node", "feat")), P(("feat", "node"), None)),
        check_vma=False,
    )
```

```python
import functools

import jax
import jax.numpy as jnp
from jax import lax
from jax.experimental import pallas as pl
from jax.experimental.pallas import tpu as pltpu
from jax.sharding import PartitionSpec as P

MESH = pl.DeviceIdType.MESH
root_half = 0.7071067811865476
inv_root_two_pi = 0.3989422804014327
RIGHT, LEFT = 0, 1
UPTO = 9
NH = 2
NEAR = (((1,), (1,)), ((), ()))
PLAIN = (((1,), (0,)), ((), ()))


def dot(left, right, dims):
    return lax.dot_general(left, right, dims, preferred_element_type=jnp.float32)


def kernel(
    nf, nn, row_ref, col_ref, blk_ref, cnt_ref, feats, weight, edges, cot, act, wgrad,
    edges_v, weight_v, cot_v, wt, adj, x, p, acc, pg, rs_out, rs_in, ng, wg_out, wg_in,
    ys, y_in, local_sem, x_recv, x_send, ag_send, ag_recv, rs_send, rs_recv,
    wg_send, wg_recv, y_send, y_recv,
):
    f, n = lax.axis_index("feat"), lax.axis_index("node")
    part = feats.shape[0]
    half = x.shape[2]
    own = 2 * half
    hid = acc.shape[0]
    hp_rows = hid // NH
    right, left = lax.rem(n + 1, nn), lax.rem(n + nn - 1, nn)

    loads = [
        pltpu.make_async_copy(edges.at[0, 0], edges_v, local_sem.at[0]),
        pltpu.make_async_copy(weight, weight_v, local_sem.at[1]),
        pltpu.make_async_copy(cot, cot_v, local_sem.at[2]),
    ]
    for copy in loads:
        copy.start()

    barrier = pltpu.get_barrier_semaphore()

    def greet_feat(i, carry):
        pl.semaphore_signal(barrier, inc=1, device_id=(lax.rem(f + i, nf), n), device_id_type=MESH)
        return carry

    def greet_node(i, carry):
        pl.semaphore_signal(barrier, inc=1, device_id=(f, lax.rem(n + i, nn)), device_id_type=MESH)
        return carry

    lax.fori_loop(1, nf, greet_feat, 0)
    lax.fori_loop(1, nn, greet_node, 0)

    own_loads = []
    for a in range(2):
        copy = pltpu.make_async_copy(
            feats.at[:, pl.ds(pl.multiple_of(f * own + a * half, half), half)],
            x.at[a, pl.ds(pl.multiple_of(f * part, part), part)],
            local_sem.at[3 + a],
        )
        copy.start()
        own_loads.append(copy)

    pl.semaphore_wait(barrier, nf + nn - 2)

    def feat_copy(a, i):
        to = lax.rem(f + i, nf)
        return pltpu.make_async_remote_copy(
            src_ref=feats.at[:, pl.ds(pl.multiple_of(to * own + a * half, half), half)],
            dst_ref=x.at[a, pl.ds(pl.multiple_of(f * part, part), part)],
            send_sem=x_send.at[a],
            recv_sem=x_recv.at[a],
            device_id=(to, n),
            device_id_type=MESH,
        )

    for a in range(2):

        def send_feat(i, carry):
            feat_copy(a, i).start()
            return carry

        lax.fori_loop(1, nf, send_feat, 0)

    def all_feats(a):
        block = x.at[a, pl.ds(0, (nf - 1) * part)]
        return pltpu.make_async_remote_copy(
            src_ref=block, dst_ref=block, send_sem=x_send.at[a], recv_sem=x_recv.at[a],
            device_id=(f, n), device_id_type=MESH,
        )

    loads[1].wait()
    wt[...] = weight_v[...].T
    loads[0].wait()
    slots = edges_v.shape[0]
    cols = 2 * nn
    count = cnt_ref[0, 0]
    for r in range(2):

        def place(c, carry):
            chosen, used = jnp.int32(0), jnp.int32(0)
            for s in range(slots):
                hit = jnp.logical_and(row_ref[0, 0, s] == r, col_ref[0, 0, s] == c)
                hit = jnp.logical_and(hit, s < count)
                chosen = chosen + jnp.where(hit, blk_ref[0, 0, s], 0)
                used = used + jnp.where(hit, 1, 0)
            block = edges_v[chosen].astype(jnp.float32)
            block = jnp.where(used > 0, block, 0.0)
            adj[c, pl.ds(r * half, half), :] = block.astype(jnp.bfloat16)
            return carry

        lax.fori_loop(0, cols, place, 0)
    loads[2].wait()

    finals = []

    def ag_len(d, a, h):
        longer = (a + h) % 2 == 0
        return 4 if longer == (d == RIGHT) else 3

    def rows_of(h):
        return pl.ds(h * hp_rows, hp_rows)

    def ag_copy(d, s, a, h, slot):
        block = p.at[slot, a, rows_of(h)]
        return pltpu.make_async_remote_copy(
            src_ref=block, dst_ref=block,
            send_sem=ag_send.at[d, s, a, h], recv_sem=ag_recv.at[d, s, a, h],
            device_id=(f, right if d == RIGHT else left), device_id_type=MESH,
        )

    def slot_at(d, s):
        return lax.rem(n + nn - s, nn) if d == RIGHT else lax.rem(n + s, nn)

    def ag_send_step(d, s, a, h):
        copy = ag_copy(d, s, a, h, slot_at(d, s))
        copy.start()
        finals.append(copy.wait_send)

    def add_block(slot, a, h, first):
        term = dot(p[slot, a, rows_of(h), :], adj[2 * slot + a], NEAR)
        if first:
            acc[rows_of(h), :] = term
        else:
            acc[rows_of(h), :] += term

    def project(a):
        all_feats(a).wait_recv()
        own_loads[a].wait()
        p[n, a] = dot(wt[...], x[a], PLAIN).astype(jnp.bfloat16)
        for h in range(NH):
            for d in (RIGHT, LEFT):
                ag_send_step(d, 0, a, h)
        for h in range(NH):
            add_block(n, a, h, a == 0)

    def ag_step(s, a, h):
        got = []
        for d in (RIGHT, LEFT):
            if s <= ag_len(d, a, h):
                ag_copy(d, s - 1, a, h, slot_at(d, s)).wait_recv()
                got.append(d)
                if s < ag_len(d, a, h):
                    ag_send_step(d, s, a, h)
        for d in got:
            add_block(slot_at(d, s), a, h, False)

    def activate(h):
        u = acc[rows_of(h), :]
        cdf = 0.5 * (1.0 + lax.erf(u * root_half))
        pdf = jnp.exp(-0.5 * u * u) * inv_root_two_pi
        act[rows_of(h), :] = (u * cdf).astype(jnp.bfloat16)
        grad = cot_v[rows_of(h), :].astype(jnp.float32) * (cdf + u * pdf)
        pg[rows_of(h), :] = grad.astype(jnp.bfloat16)

    def rs_len(d, h):
        return 4 if (h % 2 == 0) == (d == RIGHT) else 3

    def rs_copy(d, s, h):
        return pltpu.make_async_remote_copy(
            src_ref=rs_out.at[d, s, rows_of(h)], dst_ref=rs_in.at[d, s, rows_of(h)],
            send_sem=rs_send.at[d, s, h], recv_sem=rs_recv.at[d, s, h],
            device_id=(f, right if d == RIGHT else left), device_id_type=MESH,
        )

    def term(m, h):
        block = jnp.concatenate([adj[2 * m], adj[2 * m + 1]], axis=1)
        return dot(pg[rows_of(h), :], block, PLAIN)

    def rs_step(s, h):
        for d in (RIGHT, LEFT):
            away = rs_len(d, h) - s
            if away <= 0:
                continue
            m = lax.rem(n + away, nn) if d == RIGHT else lax.rem(n + nn - away, nn)
            total = term(m, h)
            if s > 0:
                rs_copy(d, s - 1, h).wait_recv()
                total = total + rs_in[d, s - 1, rows_of(h), :].astype(jnp.float32)
            rs_out[d, s, rows_of(h), :] = total.astype(jnp.bfloat16)
            copy = rs_copy(d, s, h)
            copy.start()
            finals.append(copy.wait_send)

    def rs_end(h):
        total = term(n, h)
        for d in (RIGHT, LEFT):
            rs_copy(d, rs_len(d, h) - 1, h).wait_recv()
            total = total + rs_in[d, rs_len(d, h) - 1, rows_of(h), :].astype(jnp.float32)
        ng[rows_of(h), :] = total.astype(jnp.bfloat16)

    def wg_copy(w, i):
        to = lax.rem(f + i, nf)
        return pltpu.make_async_remote_copy(
            src_ref=wg_out.at[w, to], dst_ref=wg_in.at[w, f],
            send_sem=wg_send.at[w], recv_sem=wg_recv.at[w],
            device_id=(to, n), device_id_type=MESH,
        )

    def wg_all(w):
        block = wg_in.at[w, pl.ds(0, nf - 1)]
        return pltpu.make_async_remote_copy(
            src_ref=block, dst_ref=block, send_sem=wg_send.at[w], recv_sem=wg_recv.at[w],
            device_id=(f, n), device_id_type=MESH,
        )

    def wg_start(w):
        units = pl.ds(w * 128, 128)
        quarter = nf // 4
        for q in range(4):
            features = pl.ds(q * quarter * part, quarter * part)
            block = dot(x[0, features, :], ng[units, pl.ds(0, half)], NEAR)
            block = block + dot(x[1, features, :], ng[units, pl.ds(half, half)], NEAR)
            wg_out[w, pl.ds(q * quarter, quarter)] = block.astype(jnp.bfloat16).reshape(quarter, part, 128)

        def send_wg(i, carry):
            wg_copy(w, i).start()
            return carry

        lax.fori_loop(1, nf, send_wg, 0)
        wg_in[w, f] = wg_out[w, f]

    def y_copy(w, i):
        to = lax.rem(n + i, nn)
        return pltpu.make_async_remote_copy(
            src_ref=ys.at[w, lax.div(to, 4)], dst_ref=y_in.at[w, n],
            send_sem=y_send.at[w], recv_sem=y_recv.at[w],
            device_id=(f, to), device_id_type=MESH,
        )

    def y_all(w):
        block = y_in.at[w, pl.ds(0, nn - 1)]
        return pltpu.make_async_remote_copy(
            src_ref=block, dst_ref=block, send_sem=y_send.at[w], recv_sem=y_recv.at[w],
            device_id=(f, n), device_id_type=MESH,
        )

    def wg_sum(w):
        wg_all(w).wait_recv()
        total = jnp.sum(wg_in[w].astype(jnp.float32), axis=0)
        ys[w] = total.reshape(2, 8, 128)

        def send_y(i, carry):
            y_copy(w, i).start()
            return carry

        lax.fori_loop(1, nn, send_y, 0)
        y_in[w, n] = ys[w, lax.div(n, 4)]

    def y_sum(w):
        y_all(w).wait_recv()
        total = jnp.sum(y_in[w], axis=0)
        at = lax.rem(n, 4)
        mine = total[6:8]
        for k in range(3):
            mine = jnp.where(at == k, total[2 * k : 2 * k + 2], mine)
        wgrad[:, pl.ds(w * 128, 128)] = mine

    halves = range(NH)
    if UPTO == 1:
        for a in range(2):
            all_feats(a).wait_recv()
            own_loads[a].wait()
        act[...] = x[0, 0:256, :].astype(jnp.bfloat16).repeat(2, axis=1) if False else cot_v[...]
        wgrad[...] = jnp.zeros_like(wgrad)
    if UPTO >= 2:
        project(0)
        for s in (1, 2):
            for h in halves:
                ag_step(s, 0, h)
        project(1)
        for h in halves:
            ag_step(3, 0, h)
        for h in halves:
            ag_step(1, 1, h)
        for h in halves:
            ag_step(4, 0, h)
        for s in (2, 3, 4):
            for h in halves:
                ag_step(s, 1, h)
                if s == 4:
                    activate(h)
                    if UPTO >= 3:
                        rs_step(0, h)
        if UPTO == 2:
            wgrad[...] = jnp.zeros_like(wgrad)
    if UPTO >= 3:
        for s in (1, 2, 3):
            for h in halves:
                rs_step(s, h)
        if UPTO == 3:
            for h in halves:
                rs_end(h)
            wgrad[...] = jnp.zeros_like(wgrad)
    if UPTO >= 4:
        for w in range(2):
            for h in range(w * NH // 2, (w + 1) * NH // 2):
                rs_end(h)
            wg_start(w)
        for w in range(2):
            wg_sum(w)
        for w in range(2):
            y_sum(w)
            wg_all(w).wait_send()
            y_all(w).wait_send()
    for a in range(2):
        all_feats(a).wait_send()
    for wait in finals:
        wait()


def per_device(nf, nn, feats, weight, tile_row, tile_col, tile_block, tile_count, edge_blocks, cotangent):
    fin, hid = weight.shape
    own = cotangent.shape[1]
    half = own // 2
    part = feats.shape[0]
    slots = edge_blocks.shape[2]
    bf, f32 = jnp.bfloat16, jnp.float32
    vm, dma = pltpu.VMEM, pltpu.SemaphoreType.DMA
    smem = pl.BlockSpec(memory_space=pltpu.SMEM)
    anywhere = pl.BlockSpec(memory_space=pl.ANY)
    return pl.pallas_call(
        functools.partial(kernel, nf, nn),
        out_shape=(
            jax.ShapeDtypeStruct((hid, own), bf),
            jax.ShapeDtypeStruct((fin // (nf * nn), hid), f32),
        ),
        in_specs=[smem] * 4 + [anywhere] * 4,
        out_specs=(pl.BlockSpec(memory_space=vm), pl.BlockSpec(memory_space=vm)),
        scratch_shapes=[
            vm((slots, half, half), bf),
            vm((fin, hid), bf),
            vm((hid, own), bf),
            vm((hid, fin), bf),
            vm((2 * nn, own, half), bf),
            vm((2, fin, half), bf),
            vm((nn, 2, hid, half), bf),
            vm((hid, own), f32),
            vm((hid, own), bf),
            vm((2, 4, hid, own), bf),
            vm((2, 4, hid, own), bf),
            vm((hid, own), bf),
            vm((2, nf, part, 128), bf),
            vm((2, nf, part, 128), bf),
            vm((2, 2, 8, 128), f32),
            vm((2, nn, 8, 128), f32),
            dma((5,)),
            dma((2,)),
            dma((2,)),
            dma((2, 4, 2, NH)),
            dma((2, 4, 2, NH)),
            dma((2, 4, NH)),
            dma((2, 4, NH)),
            dma((2,)),
            dma((2,)),
            dma((2,)),
            dma((2,)),
        ],
        compiler_params=pltpu.CompilerParams(
            collective_id=0, has_side_effects=True, vmem_limit_bytes=40 * 1024 * 1024
        ),
        name="graphconv",
    )(tile_row, tile_col, tile_block, tile_count, feats, weight, edge_blocks, cotangent)


def solution(mesh):
    return jax.shard_map(
        functools.partial(per_device, mesh.shape["feat"], mesh.shape["node"]),
        mesh=mesh,
        in_specs=(
            P("feat", "node"),
            P(),
            P("feat", "node", None),
            P("feat", "node", None),
            P("feat", "node", None),
            P("feat", "node"),
            P("feat", "node", None, None, None),
            P(None, ("node", "feat")),
        ),
        out_specs=(P(None, ("node", "feat")), P(("feat", "node"), None)),
        check_vma=False,
    )
```

```python
import functools

import jax
import jax.numpy as jnp
from jax import lax
from jax.experimental import pallas as pl
from jax.experimental.pallas import tpu as pltpu
from jax.sharding import PartitionSpec as P

MESH = pl.DeviceIdType.MESH
root_half = 0.7071067811865476
inv_root_two_pi = 0.3989422804014327
RIGHT, LEFT = 0, 1
NH = 4
ORDER = (2, 1, 3, 4)
AG_TREE = {1: 0, 2: 0, 3: 2, 4: 2}
RS_TREE = {1: 0, 2: 1, 3: 2, 4: 2}
NEAR = (((1,), (1,)), ((), ()))
PLAIN = (((1,), (0,)), ((), ()))


def dot(left, right, dims):
    return lax.dot_general(left, right, dims, preferred_element_type=jnp.float32)


def kernel(
    nf, nn, row_any, col_any, blk_any, cnt_ref, feats, weight, edges, cot, act, wgrad,
    row_ref, col_ref, blk_ref, edges_v, weight_v, cot_v, feats_v, fs, wt, adj, x, p, acc, pg,
    rs_out, rs_in, ng, wg_out, wg_in, ys, y_in, local_sem, x_recv, x_send, ag_send, ag_recv, rs_send,
    rs_recv, wg_send, wg_recv, y_send, y_recv,
):
    f, n = lax.axis_index("feat"), lax.axis_index("node")
    part = feats.shape[0]
    half = x.shape[2]
    own = 2 * half
    hid = acc.shape[0]
    hp_rows = hid // NH
    right, left = lax.rem(n + 1, nn), lax.rem(n + nn - 1, nn)

    nz = nn
    fx, fz, fc = lax.div(f, 2 * nz), lax.rem(lax.div(f, 2), nz), lax.rem(f, 2)
    group = 2 * fx + fc
    groups = nf // nz

    def feat_of(g, z):
        return lax.div(g, 2) * (2 * nz) + z * 2 + lax.rem(g, 2)

    loads = [
        pltpu.make_async_copy(feats, feats_v, local_sem.at[3]),
        pltpu.make_async_copy(weight, weight_v, local_sem.at[1]),
        pltpu.make_async_copy(edges.at[0, 0], edges_v, local_sem.at[0]),
        pltpu.make_async_copy(cot, cot_v, local_sem.at[2]),
        pltpu.make_async_copy(row_any, row_ref, local_sem.at[4]),
        pltpu.make_async_copy(col_any, col_ref, local_sem.at[5]),
        pltpu.make_async_copy(blk_any, blk_ref, local_sem.at[6]),
    ]
    for copy in loads:
        copy.start()

    barrier = pltpu.get_barrier_semaphore()

    def greet_feat(i, carry):
        pl.semaphore_signal(barrier, inc=1, device_id=(lax.rem(f + i, nf), n), device_id_type=MESH)
        return carry

    def greet_node(i, carry):
        z = lax.rem(i, nz)
        to = lax.rem(n + lax.div(i, nz), nn)
        pl.semaphore_signal(barrier, inc=1, device_id=(feat_of(group, z), to), device_id_type=MESH)
        return carry

    lax.fori_loop(1, nf, greet_feat, 0)
    lax.fori_loop(nz, nz * nn, greet_node, 0)

    loads[0].wait()

    def spread(t, carry):
        for a in range(2):
            fs[a, t] = feats_v[:, pl.ds(pl.multiple_of(t * own + a * half, half), half)]
        return carry

    lax.fori_loop(0, nf, spread, 0)
    for a in range(2):
        x[a, pl.ds(pl.multiple_of(f * part, part), part), :] = fs[a, f]

    pl.semaphore_wait(barrier, nf - 1 + nz * (nn - 1))

    def feat_copy(a, i):
        to = lax.rem(f + i, nf)
        return pltpu.make_async_remote_copy(
            src_ref=fs.at[a, to],
            dst_ref=x.at[a, pl.ds(pl.multiple_of(f * part, part), part)],
            send_sem=x_send.at[a],
            recv_sem=x_recv.at[a],
            device_id=(to, n),
            device_id_type=MESH,
        )

    for a in range(2):

        def send_feat(i, carry):
            feat_copy(a, i).start()
            return carry

        lax.fori_loop(1, nf, send_feat, 0)

    def all_feats(a):
        block = x.at[a, pl.ds(0, (nf - 1) * part)]
        return pltpu.make_async_remote_copy(
            src_ref=block, dst_ref=block, send_sem=x_send.at[a], recv_sem=x_recv.at[a],
            device_id=(f, n), device_id_type=MESH,
        )

    loads[1].wait()
    wt[...] = weight_v[...].T
    for k in (2, 4, 5, 6):
        loads[k].wait()
    slots = edges_v.shape[0]
    cols = 2 * nn
    count = cnt_ref[0, 0]
    for r in range(2):

        def place(c, carry):
            chosen, used = jnp.int32(0), jnp.int32(0)
            for s in range(slots):
                hit = jnp.logical_and(row_ref[0, 0, s] == r, col_ref[0, 0, s] == c)
                hit = jnp.logical_and(hit, s < count)
                chosen = chosen + jnp.where(hit, blk_ref[0, 0, s], 0)
                used = used + jnp.where(hit, 1, 0)
            block = edges_v[chosen].astype(jnp.float32)
            block = jnp.where(used > 0, block, 0.0)
            adj[c, pl.ds(r * half, half), :] = block.astype(jnp.bfloat16)
            return carry

        lax.fori_loop(0, cols, place, 0)
    loads[3].wait()

    finals = []

    def ag_len(d, a, h):
        longer = (a + h) % 2 == 0
        return 4 if longer == (d == RIGHT) else 3

    def rows_of(h):
        return pl.ds(h * hp_rows, hp_rows)

    def slot_at(d, s):
        return lax.rem(n + nn - s, nn) if d == RIGHT else lax.rem(n + s, nn)

    def to_node(d, hop):
        return lax.rem(n + hop, nn) if d == RIGHT else lax.rem(n + nn - hop, nn)

    def ag_copy(d, at, hop, a, h):
        block = p.at[slot_at(d, at), a, rows_of(h)]
        return pltpu.make_async_remote_copy(
            src_ref=block, dst_ref=block,
            send_sem=ag_send.at[d, at + hop - 1, a, h], recv_sem=ag_recv.at[d, at + hop - 1, a, h],
            device_id=(f, to_node(d, hop)), device_id_type=MESH,
        )

    def ag_pass(d, at, a, h):
        for k in sorted(AG_TREE, reverse=True):
            if AG_TREE[k] == at and k <= ag_len(d, a, h):
                copy = ag_copy(d, at, k - at, a, h)
                copy.start()
                finals.append(copy.wait_send)

    def add_block(slot, a, h, first):
        term = dot(p[slot, a, rows_of(h), :], adj[2 * slot + a], NEAR)
        if first:
            acc[rows_of(h), :] = term
        else:
            acc[rows_of(h), :] += term

    def project(a):
        all_feats(a).wait_recv()
        p[n, a] = dot(wt[...], x[a], PLAIN).astype(jnp.bfloat16)
        for h in range(NH):
            for d in (RIGHT, LEFT):
                ag_pass(d, 0, a, h)
        for h in range(NH):
            add_block(n, a, h, a == 0)

    def ag_step(k, a, h):
        got = [d for d in (RIGHT, LEFT) if k <= ag_len(d, a, h)]
        for d in got:
            block = p.at[slot_at(d, k), a, rows_of(h)]
            pltpu.make_async_remote_copy(
                src_ref=block, dst_ref=block,
                send_sem=ag_send.at[d, k - 1, a, h], recv_sem=ag_recv.at[d, k - 1, a, h],
                device_id=(f, n), device_id_type=MESH,
            ).wait_recv()
            ag_pass(d, k, a, h)
        for d in got:
            add_block(slot_at(d, k), a, h, False)

    def activate(h):
        u = acc[rows_of(h), :]
        cdf = 0.5 * (1.0 + lax.erf(u * root_half))
        pdf = jnp.exp(-0.5 * u * u) * inv_root_two_pi
        act[rows_of(h), :] = (u * cdf).astype(jnp.bfloat16)
        grad = cot_v[rows_of(h), :].astype(jnp.float32) * (cdf + u * pdf)
        pg[rows_of(h), :] = grad.astype(jnp.bfloat16)

    def rs_len(d, h):
        return 4 if (h % 2 == 0) == (d == RIGHT) else 3

    def rs_copy(d, k, h):
        return pltpu.make_async_remote_copy(
            src_ref=rs_out.at[d, k - 1, rows_of(h)], dst_ref=rs_in.at[d, k - 1, rows_of(h)],
            send_sem=rs_send.at[d, k - 1, h], recv_sem=rs_recv.at[d, k - 1, h],
            device_id=(f, to_node(d, k - RS_TREE[k])), device_id_type=MESH,
        )

    def rs_add(total, d, k, h):
        for j in sorted(RS_TREE):
            if RS_TREE[j] == k and j <= rs_len(d, h):
                rs_copy(d, j, h).wait_recv()
                total = total + rs_in[d, j - 1, rows_of(h), :].astype(jnp.float32)
        return total

    def term(m, h):
        block = jnp.concatenate([adj[2 * m], adj[2 * m + 1]], axis=1)
        return dot(pg[rows_of(h), :], block, PLAIN)

    def rs_step(k, h):
        for d in (RIGHT, LEFT):
            if k > rs_len(d, h):
                continue
            total = rs_add(term(to_node(d, k), h), d, k, h)
            rs_out[d, k - 1, rows_of(h), :] = total.astype(jnp.bfloat16)
            copy = rs_copy(d, k, h)
            copy.start()
            finals.append(copy.wait_send)

    def rs_end(h):
        total = term(n, h)
        for d in (RIGHT, LEFT):
            total = rs_add(total, d, 0, h)
        ng[rows_of(h), :] = total.astype(jnp.bfloat16)

    def wg_copy(w, i):
        to = lax.rem(group + i, groups)
        return pltpu.make_async_remote_copy(
            src_ref=wg_out.at[w, to], dst_ref=wg_in.at[w, group],
            send_sem=wg_send.at[w], recv_sem=wg_recv.at[w],
            device_id=(feat_of(to, fz), n), device_id_type=MESH,
        )

    def wg_all(w):
        block = wg_in.at[w, pl.ds(0, groups - 1)]
        return pltpu.make_async_remote_copy(
            src_ref=block, dst_ref=block, send_sem=wg_send.at[w], recv_sem=wg_recv.at[w],
            device_id=(f, n), device_id_type=MESH,
        )

    def wg_start(w):
        units = pl.ds(w * 128, 128)
        rows = 2 * nz * part
        for q in range(groups // 2):
            features = pl.ds(q * rows, rows)
            block = dot(x[0, features, :], ng[units, pl.ds(0, half)], NEAR)
            block = block + dot(x[1, features, :], ng[units, pl.ds(half, half)], NEAR)
            block = block.astype(jnp.bfloat16).reshape(nz, 2, part, 128)
            for c in range(2):
                wg_out[w, 2 * q + c] = block[:, c]
        for i in range(1, groups):
            wg_copy(w, i).start()
        wg_in[w, group] = wg_out[w, group]

    def y_copy(w, i):
        z = lax.rem(fz + lax.rem(i, nz), nz)
        to = lax.rem(n + lax.div(i, nz), nn)
        return pltpu.make_async_remote_copy(
            src_ref=ys.at[w, z, to], dst_ref=y_in.at[w, fz * nn + n],
            send_sem=y_send.at[w], recv_sem=y_recv.at[w],
            device_id=(feat_of(group, z), to), device_id_type=MESH,
        )

    def y_all(w):
        block = y_in.at[w, pl.ds(0, nz * nn - 1)]
        return pltpu.make_async_remote_copy(
            src_ref=block, dst_ref=block, send_sem=y_send.at[w], recv_sem=y_recv.at[w],
            device_id=(f, n), device_id_type=MESH,
        )

    def wg_sum(w):
        wg_all(w).wait_recv()
        total = jnp.sum(wg_in[w].astype(jnp.float32), axis=0)
        for k in range(nn):
            ys[w, :, k] = total[:, 2 * k : 2 * k + 2]

        def send_y(i, carry):
            y_copy(w, i).start()
            return carry

        lax.fori_loop(1, nz * nn, send_y, 0)
        y_in[w, fz * nn + n] = ys[w, fz, n]

    def y_sum(w):
        y_all(w).wait_recv()
        wgrad[:, pl.ds(w * 128, 128)] = jnp.sum(y_in[w], axis=0)

    halves = range(NH)
    project(0)
    for k in ORDER[:2]:
        for h in halves:
            ag_step(k, 0, h)
    project(1)
    for h in halves:
        ag_step(ORDER[0], 1, h)
    for h in halves:
        ag_step(ORDER[2], 0, h)
    for h in halves:
        ag_step(ORDER[1], 1, h)
    for h in halves:
        ag_step(ORDER[3], 0, h)
    for h in halves:
        ag_step(ORDER[2], 1, h)
        ag_step(ORDER[3], 1, h)
        activate(h)
        for k in (4, 3):
            if k not in RS_TREE.values():
                rs_step(k, h)
    for k in (3, 2, 1):
        if k in RS_TREE.values() or k < 3:
            for h in halves:
                rs_step(k, h)
    for w in range(2):
        for h in range(w * NH // 2, (w + 1) * NH // 2):
            rs_end(h)
        wg_start(w)
    for w in range(2):
        wg_sum(w)
    for w in range(2):
        y_sum(w)
        wg_all(w).wait_send()
        y_all(w).wait_send()
    for a in range(2):
        all_feats(a).wait_send()
    for wait in finals:
        wait()


def per_device(nf, nn, feats, weight, tile_row, tile_col, tile_block, tile_count, edge_blocks, cotangent):
    fin, hid = weight.shape
    own = cotangent.shape[1]
    half = own // 2
    part = feats.shape[0]
    slots = edge_blocks.shape[2]
    bf, f32 = jnp.bfloat16, jnp.float32
    vm, dma = pltpu.VMEM, pltpu.SemaphoreType.DMA
    smem = pltpu.SMEM
    anywhere = pl.BlockSpec(memory_space=pltpu.HBM)
    return pl.pallas_call(
        functools.partial(kernel, nf, nn),
        out_shape=(
            jax.ShapeDtypeStruct((hid, own), bf),
            jax.ShapeDtypeStruct((fin // (nf * nn), hid), f32),
        ),
        in_specs=[anywhere] * 3 + [pl.BlockSpec(memory_space=smem)] + [anywhere] * 4,
        out_specs=(pl.BlockSpec(memory_space=vm), pl.BlockSpec(memory_space=vm)),
        scratch_shapes=[
            smem(tile_row.shape, jnp.int32),
            smem(tile_col.shape, jnp.int32),
            smem(tile_block.shape, jnp.int32),
            vm((slots, half, half), bf),
            vm((fin, hid), bf),
            vm((hid, own), bf),
            vm(feats.shape, bf),
            vm((2, nf, part, half), bf),
            vm((hid, fin), bf),
            vm((2 * nn, own, half), bf),
            vm((2, fin, half), bf),
            vm((nn, 2, hid, half), bf),
            vm((hid, own), f32),
            vm((hid, own), bf),
            vm((2, 4, hid, own), bf),
            vm((2, 4, hid, own), bf),
            vm((hid, own), bf),
            vm((2, nf // nn, nn, part, 128), bf),
            vm((2, nf // nn, nn, part, 128), bf),
            vm((2, nn, nn, 2, 128), f32),
            vm((2, nn * nn, 2, 128), f32),
            dma((7,)),
            dma((2,)),
            dma((2,)),
            dma((2, 4, 2, NH)),
            dma((2, 4, 2, NH)),
            dma((2, 4, NH)),
            dma((2, 4, NH)),
            dma((2,)),
            dma((2,)),
            dma((2,)),
            dma((2,)),
        ],
        compiler_params=pltpu.CompilerParams(
            collective_id=0, has_side_effects=True, vmem_limit_bytes=40 * 1024 * 1024
        ),
        name="graphconv",
    )(*[stay(v) for v in (tile_row, tile_col, tile_block)], tile_count, *[stay(v) for v in (feats, weight, edge_blocks, cotangent)])


def stay(array):
    return pltpu.with_memory_space_constraint(array, pltpu.HBM)


def solution(mesh):
    return jax.shard_map(
        functools.partial(per_device, mesh.shape["feat"], mesh.shape["node"]),
        mesh=mesh,
        in_specs=(
            P("feat", "node"),
            P(),
            P("feat", "node", None),
            P("feat", "node", None),
            P("feat", "node", None),
            P("feat", "node"),
            P("feat", "node", None, None, None),
            P(None, ("node", "feat")),
        ),
        out_specs=(P(None, ("node", "feat")), P(("feat", "node"), None)),
        check_vma=False,
    )
```

```python
import functools

import jax
import jax.numpy as jnp
from jax import lax
from jax.experimental import pallas as pl
from jax.experimental.pallas import tpu as pltpu
from jax.sharding import PartitionSpec as P

MESH = pl.DeviceIdType.MESH
root_half = 0.7071067811865476
inv_root_two_pi = 0.3989422804014327
RIGHT, LEFT = 0, 1
NH = 4
ORDER = (2, 1, 3, 4)
AG_TREE = {1: 0, 2: 0, 3: 2, 4: 2}
RS_TREE = {1: 0, 2: 1, 3: 2, 4: 2}
NEAR = (((1,), (1,)), ((), ()))
PLAIN = (((1,), (0,)), ((), ()))


def dot(left, right, dims):
    return lax.dot_general(left, right, dims, preferred_element_type=jnp.float32)


def kernel(
    nf, nn, row_any, col_any, blk_any, cnt_ref, feats, weight, edges, cot, act, wgrad,
    row_ref, col_ref, blk_ref, edges_v, weight_v, cot_v, feats_v, fs, wt, adj, x, p, acc, pg,
    rs_out, rs_in, ng, wg_out, wg_in, ys, y_in, local_sem, x_recv, x_send, ag_send, ag_recv, rs_send,
    rs_recv, wg_send, wg_recv, y_send, y_recv,
):
    f, n = lax.axis_index("feat"), lax.axis_index("node")
    part = feats.shape[0]
    half = x.shape[2]
    own = 2 * half
    hid = acc.shape[0]
    hp_rows = hid // NH
    right, left = lax.rem(n + 1, nn), lax.rem(n + nn - 1, nn)

    nz = nn
    fx, fz, fc = lax.div(f, 2 * nz), lax.rem(lax.div(f, 2), nz), lax.rem(f, 2)
    group = 2 * fx + fc
    groups = nf // nz

    def feat_of(g, z):
        return lax.div(g, 2) * (2 * nz) + z * 2 + lax.rem(g, 2)

    loads = [
        pltpu.make_async_copy(feats, feats_v, local_sem.at[3]),
        pltpu.make_async_copy(weight, weight_v, local_sem.at[1]),
        pltpu.make_async_copy(edges.at[0, 0], edges_v, local_sem.at[0]),
        pltpu.make_async_copy(cot, cot_v, local_sem.at[2]),
        pltpu.make_async_copy(row_any, row_ref, local_sem.at[4]),
        pltpu.make_async_copy(col_any, col_ref, local_sem.at[5]),
        pltpu.make_async_copy(blk_any, blk_ref, local_sem.at[6]),
    ]
    for copy in loads:
        copy.start()

    barrier = pltpu.get_barrier_semaphore()

    def greet_feat(i, carry):
        pl.semaphore_signal(barrier, inc=1, device_id=(lax.rem(f + i, nf), n), device_id_type=MESH)
        return carry

    def greet_node(i, carry):
        z = lax.rem(i, nz)
        to = lax.rem(n + lax.div(i, nz), nn)
        pl.semaphore_signal(barrier, inc=1, device_id=(feat_of(group, z), to), device_id_type=MESH)
        return carry

    lax.fori_loop(1, nf, greet_feat, 0)
    lax.fori_loop(nz, nz * nn, greet_node, 0)

    loads[0].wait()

    def spread(t, carry):
        for a in range(2):
            fs[a, t] = feats_v[:, pl.ds(pl.multiple_of(t * own + a * half, half), half)]
        return carry

    lax.fori_loop(0, nf, spread, 0)
    for a in range(2):
        x[a, pl.ds(pl.multiple_of(f * part, part), part), :] = fs[a, f]

    pl.semaphore_wait(barrier, nf - 1 + nz * (nn - 1))

    def feat_copy(a, to):
        return pltpu.make_async_remote_copy(
            src_ref=fs.at[a, to],
            dst_ref=x.at[a, pl.ds(pl.multiple_of(f * part, part), part)],
            send_sem=x_send.at[a],
            recv_sem=x_recv.at[a],
            device_id=(to, n),
            device_id_type=MESH,
        )

    for a in range(2):

        def send_feat(i, carry):
            feat_copy(a, lax.rem(f + i, nf)).start()
            return carry

        lax.fori_loop(1, nf, send_feat, 0)

    def all_feats(a):
        block = x.at[a, pl.ds(0, (nf - 1) * part)]
        return pltpu.make_async_remote_copy(
            src_ref=block, dst_ref=block, send_sem=x_send.at[a], recv_sem=x_recv.at[a],
            device_id=(f, n), device_id_type=MESH,
        )

    loads[1].wait()
    wt[...] = weight_v[...].T
    for k in (2, 4, 5, 6):
        loads[k].wait()
    slots = edges_v.shape[0]
    cols = 2 * nn
    count = cnt_ref[0, 0]
    for r in range(2):

        def place(c, carry):
            chosen, used = jnp.int32(0), jnp.int32(0)
            for s in range(slots):
                hit = jnp.logical_and(row_ref[0, 0, s] == r, col_ref[0, 0, s] == c)
                hit = jnp.logical_and(hit, s < count)
                chosen = chosen + jnp.where(hit, blk_ref[0, 0, s], 0)
                used = used + jnp.where(hit, 1, 0)
            block = edges_v[chosen].astype(jnp.float32)
            block = jnp.where(used > 0, block, 0.0)
            adj[c, pl.ds(r * half, half), :] = block.astype(jnp.bfloat16)
            return carry

        lax.fori_loop(0, cols, place, 0)
    loads[3].wait()

    finals = []

    def ag_len(d, a, h):
        longer = (a + h) % 2 == 0
        return 4 if longer == (d == RIGHT) else 3

    def rows_of(h):
        return pl.ds(h * hp_rows, hp_rows)

    def slot_at(d, s):
        return lax.rem(n + nn - s, nn) if d == RIGHT else lax.rem(n + s, nn)

    def to_node(d, hop):
        return lax.rem(n + hop, nn) if d == RIGHT else lax.rem(n + nn - hop, nn)

    def ag_copy(d, at, hop, a, h):
        block = p.at[slot_at(d, at), a, rows_of(h)]
        return pltpu.make_async_remote_copy(
            src_ref=block, dst_ref=block,
            send_sem=ag_send.at[d, at + hop - 1, a, h], recv_sem=ag_recv.at[d, at + hop - 1, a, h],
            device_id=(f, to_node(d, hop)), device_id_type=MESH,
        )

    def ag_pass(d, at, a, h, chosen=(4, 3, 2, 1)):
        for k in chosen:
            if AG_TREE[k] == at and k <= ag_len(d, a, h):
                copy = ag_copy(d, at, k - at, a, h)
                copy.start()
                finals.append(copy.wait_send)

    def add_block(slot, a, h, first):
        term = dot(p[slot, a, rows_of(h), :], adj[2 * slot + a], NEAR)
        if first:
            acc[rows_of(h), :] = term
        else:
            acc[rows_of(h), :] += term

    def project(a):
        all_feats(a).wait_recv()
        for w in range(2):
            rows = pl.ds(w * 128, 128)
            p[n, a, rows, :] = dot(wt[rows, :], x[a], PLAIN).astype(jnp.bfloat16)
            for h in range(w * NH // 2, (w + 1) * NH // 2):
                for d in (RIGHT, LEFT):
                    ag_pass(d, 0, a, h, (4, 3, 2))
        for h in range(NH):
            for d in (RIGHT, LEFT):
                ag_pass(d, 0, a, h, (1,))
        for h in range(NH):
            add_block(n, a, h, a == 0)

    def ag_step(k, a, h):
        got = [d for d in (RIGHT, LEFT) if k <= ag_len(d, a, h)]
        for d in got:
            block = p.at[slot_at(d, k), a, rows_of(h)]
            pltpu.make_async_remote_copy(
                src_ref=block, dst_ref=block,
                send_sem=ag_send.at[d, k - 1, a, h], recv_sem=ag_recv.at[d, k - 1, a, h],
                device_id=(f, n), device_id_type=MESH,
            ).wait_recv()
            ag_pass(d, k, a, h)
        for d in got:
            add_block(slot_at(d, k), a, h, False)

    def activate(h):
        u = acc[rows_of(h), :]
        cdf = 0.5 * (1.0 + lax.erf(u * root_half))
        pdf = jnp.exp(-0.5 * u * u) * inv_root_two_pi
        act[rows_of(h), :] = (u * cdf).astype(jnp.bfloat16)
        grad = cot_v[rows_of(h), :].astype(jnp.float32) * (cdf + u * pdf)
        pg[rows_of(h), :] = grad.astype(jnp.bfloat16)

    def rs_len(d, h):
        return 4 if (h % 2 == 0) == (d == RIGHT) else 3

    def rs_copy(d, k, h):
        return pltpu.make_async_remote_copy(
            src_ref=rs_out.at[d, k - 1, rows_of(h)], dst_ref=rs_in.at[d, k - 1, rows_of(h)],
            send_sem=rs_send.at[d, k - 1, h], recv_sem=rs_recv.at[d, k - 1, h],
            device_id=(f, to_node(d, k - RS_TREE[k])), device_id_type=MESH,
        )

    def rs_add(total, d, k, h):
        for j in sorted(RS_TREE):
            if RS_TREE[j] == k and j <= rs_len(d, h):
                rs_copy(d, j, h).wait_recv()
                total = total + rs_in[d, j - 1, rows_of(h), :].astype(jnp.float32)
        return total

    def term(m, h):
        block = jnp.concatenate([adj[2 * m], adj[2 * m + 1]], axis=1)
        return dot(pg[rows_of(h), :], block, PLAIN)

    def rs_step(k, h):
        for d in (RIGHT, LEFT):
            if k > rs_len(d, h):
                continue
            total = rs_add(term(to_node(d, k), h), d, k, h)
            rs_out[d, k - 1, rows_of(h), :] = total.astype(jnp.bfloat16)
            copy = rs_copy(d, k, h)
            copy.start()
            finals.append(copy.wait_send)

    def rs_end(h):
        total = term(n, h)
        for d in (RIGHT, LEFT):
            total = rs_add(total, d, 0, h)
        ng[rows_of(h), :] = total.astype(jnp.bfloat16)

    def wg_copy(w, i):
        to = lax.rem(group + i, groups)
        return pltpu.make_async_remote_copy(
            src_ref=wg_out.at[w, to], dst_ref=wg_in.at[w, group],
            send_sem=wg_send.at[w], recv_sem=wg_recv.at[w],
            device_id=(feat_of(to, fz), n), device_id_type=MESH,
        )

    def wg_all(w):
        block = wg_in.at[w, pl.ds(0, groups - 1)]
        return pltpu.make_async_remote_copy(
            src_ref=block, dst_ref=block, send_sem=wg_send.at[w], recv_sem=wg_recv.at[w],
            device_id=(f, n), device_id_type=MESH,
        )

    def wg_start(w):
        units = pl.ds(w * 128, 128)
        rows = 2 * nz * part
        for q in range(groups // 2):
            features = pl.ds(q * rows, rows)
            block = dot(x[0, features, :], ng[units, pl.ds(0, half)], NEAR)
            block = block + dot(x[1, features, :], ng[units, pl.ds(half, half)], NEAR)
            block = block.astype(jnp.bfloat16).reshape(nz, 2, part, 128)
            for c in range(2):
                wg_out[w, 2 * q + c] = block[:, c]
        for i in range(1, groups):
            wg_copy(w, i).start()
        wg_in[w, group] = wg_out[w, group]

    def y_copy(i):
        z = lax.rem(fz + lax.rem(i, nz), nz)
        to = lax.rem(n + lax.div(i, nz), nn)
        return pltpu.make_async_remote_copy(
            src_ref=ys.at[z, to], dst_ref=y_in.at[fz * nn + n],
            send_sem=y_send.at[0], recv_sem=y_recv.at[0],
            device_id=(feat_of(group, z), to), device_id_type=MESH,
        )

    def y_all():
        block = y_in.at[pl.ds(0, nz * nn - 1)]
        return pltpu.make_async_remote_copy(
            src_ref=block, dst_ref=block, send_sem=y_send.at[0], recv_sem=y_recv.at[0],
            device_id=(f, n), device_id_type=MESH,
        )

    def wg_sum(w):
        wg_all(w).wait_recv()
        total = jnp.sum(wg_in[w].astype(jnp.float32), axis=0)
        for k in range(nn):
            ys[:, k, w] = total[:, 2 * k : 2 * k + 2]

    def y_exchange():
        def send_y(i, carry):
            y_copy(i).start()
            return carry

        lax.fori_loop(1, nz * nn, send_y, 0)
        y_in[fz * nn + n] = ys[fz, n]
        y_all().wait_recv()
        total = jnp.sum(y_in[...], axis=0)
        for w in range(2):
            wgrad[:, pl.ds(w * 128, 128)] = total[w]

    halves = range(NH)
    project(0)
    for k in ORDER[:2]:
        for h in halves:
            ag_step(k, 0, h)
    project(1)
    for h in halves:
        ag_step(ORDER[0], 1, h)
    for h in halves:
        ag_step(ORDER[2], 0, h)
    for h in halves:
        ag_step(ORDER[1], 1, h)
    for h in halves:
        ag_step(ORDER[3], 0, h)
    for h in halves:
        ag_step(ORDER[2], 1, h)
        ag_step(ORDER[3], 1, h)
        activate(h)
        for k in (4, 3):
            if k not in RS_TREE.values():
                rs_step(k, h)
    for k in (3, 2, 1):
        if k in RS_TREE.values() or k < 3:
            for h in halves:
                rs_step(k, h)
    for w in range(2):
        for h in range(w * NH // 2, (w + 1) * NH // 2):
            rs_end(h)
        wg_start(w)
    for w in range(2):
        wg_sum(w)
    y_exchange()
    for w in range(2):
        wg_all(w).wait_send()
    y_all().wait_send()
    for a in range(2):
        all_feats(a).wait_send()
    for wait in finals:
        wait()


def per_device(nf, nn, feats, weight, tile_row, tile_col, tile_block, tile_count, edge_blocks, cotangent):
    fin, hid = weight.shape
    own = cotangent.shape[1]
    half = own // 2
    part = feats.shape[0]
    slots = edge_blocks.shape[2]
    bf, f32 = jnp.bfloat16, jnp.float32
    vm, dma = pltpu.VMEM, pltpu.SemaphoreType.DMA
    smem = pltpu.SMEM
    anywhere = pl.BlockSpec(memory_space=pltpu.HBM)
    return pl.pallas_call(
        functools.partial(kernel, nf, nn),
        out_shape=(
            jax.ShapeDtypeStruct((hid, own), bf),
            jax.ShapeDtypeStruct((fin // (nf * nn), hid), f32),
        ),
        in_specs=[anywhere] * 3 + [pl.BlockSpec(memory_space=smem)] + [anywhere] * 4,
        out_specs=(pl.BlockSpec(memory_space=vm), pl.BlockSpec(memory_space=vm)),
        scratch_shapes=[
            smem(tile_row.shape, jnp.int32),
            smem(tile_col.shape, jnp.int32),
            smem(tile_block.shape, jnp.int32),
            vm((slots, half, half), bf),
            vm((fin, hid), bf),
            vm((hid, own), bf),
            vm(feats.shape, bf),
            vm((2, nf, part, half), bf),
            vm((hid, fin), bf),
            vm((2 * nn, own, half), bf),
            vm((2, fin, half), bf),
            vm((nn, 2, hid, half), bf),
            vm((hid, own), f32),
            vm((hid, own), bf),
            vm((2, 4, hid, own), bf),
            vm((2, 4, hid, own), bf),
            vm((hid, own), bf),
            vm((2, nf // nn, nn, part, 128), bf),
            vm((2, nf // nn, nn, part, 128), bf),
            vm((nn, nn, 2, 2, 128), f32),
            vm((nn * nn, 2, 2, 128), f32),
            dma((7,)),
            dma((2,)),
            dma((2,)),
            dma((2, 4, 2, NH)),
            dma((2, 4, 2, NH)),
            dma((2, 4, NH)),
            dma((2, 4, NH)),
            dma((2,)),
            dma((2,)),
            dma((2,)),
            dma((2,)),
        ],
        compiler_params=pltpu.CompilerParams(
            collective_id=0, has_side_effects=True, vmem_limit_bytes=40 * 1024 * 1024
        ),
        name="graphconv",
    )(*[stay(v) for v in (tile_row, tile_col, tile_block)], tile_count, *[stay(v) for v in (feats, weight, edge_blocks, cotangent)])


def stay(array):
    return pltpu.with_memory_space_constraint(array, pltpu.HBM)


def solution(mesh):
    return jax.shard_map(
        functools.partial(per_device, mesh.shape["feat"], mesh.shape["node"]),
        mesh=mesh,
        in_specs=(
            P("feat", "node"),
            P(),
            P("feat", "node", None),
            P("feat", "node", None),
            P("feat", "node", None),
            P("feat", "node"),
            P("feat", "node", None, None, None),
            P(None, ("node", "feat")),
        ),
        out_specs=(P(None, ("node", "feat")), P(("feat", "node"), None)),
        check_vma=False,
    )
```

```python
import functools

import jax
import jax.numpy as jnp
from jax import lax
from jax.experimental import pallas as pl
from jax.experimental.pallas import tpu as pltpu
from jax.sharding import PartitionSpec as P

MESH = pl.DeviceIdType.MESH
root_half = 0.7071067811865476
inv_root_two_pi = 0.3989422804014327
RIGHT, LEFT = 0, 1
NH = 4
ORDER = (2, 1, 3, 4)
AG_TREE = {1: 0, 2: 0, 3: 2, 4: 2}
RS_TREE = {1: 0, 2: 1, 3: 2, 4: 2}
NEAR = (((1,), (1,)), ((), ()))
PLAIN = (((1,), (0,)), ((), ()))


def dot(left, right, dims):
    return lax.dot_general(left, right, dims, preferred_element_type=jnp.float32)


def kernel(
    nf, nn, row_any, col_any, blk_any, cnt_ref, feats, weight, edges, cot, act, wgrad,
    row_ref, col_ref, blk_ref, edges_v, weight_v, cot_v, feats_v, fs, wt, adj, x, p, acc, pg,
    rs_out, rs_in, ng, wg_out, wg_in, ys, y_in, local_sem, x_recv, x_send, ag_send, ag_recv, rs_send,
    rs_recv, wg_send, wg_recv, y_send, y_recv,
):
    f, n = lax.axis_index("feat"), lax.axis_index("node")
    part = feats.shape[0]
    half = x.shape[2]
    own = 2 * half
    hid = acc.shape[0]
    hp_rows = hid // NH
    right, left = lax.rem(n + 1, nn), lax.rem(n + nn - 1, nn)

    nz = nn
    fx, fz, fc = lax.div(f, 2 * nz), lax.rem(lax.div(f, 2), nz), lax.rem(f, 2)
    group = 2 * fx + fc
    groups = nf // nz

    def feat_of(g, z):
        return lax.div(g, 2) * (2 * nz) + z * 2 + lax.rem(g, 2)

    loads = [
        pltpu.make_async_copy(feats, feats_v, local_sem.at[3]),
        pltpu.make_async_copy(weight, weight_v, local_sem.at[1]),
        pltpu.make_async_copy(edges.at[0, 0], edges_v, local_sem.at[0]),
        pltpu.make_async_copy(cot, cot_v, local_sem.at[2]),
        pltpu.make_async_copy(row_any, row_ref, local_sem.at[4]),
        pltpu.make_async_copy(col_any, col_ref, local_sem.at[5]),
        pltpu.make_async_copy(blk_any, blk_ref, local_sem.at[6]),
    ]
    for copy in loads:
        copy.start()

    barrier = pltpu.get_barrier_semaphore()

    def greet_feat(i, carry):
        pl.semaphore_signal(barrier, inc=1, device_id=(lax.rem(f + i, nf), n), device_id_type=MESH)
        return carry

    def greet_node(i, carry):
        z = lax.rem(i, nz)
        to = lax.rem(n + lax.div(i, nz), nn)
        pl.semaphore_signal(barrier, inc=1, device_id=(feat_of(group, z), to), device_id_type=MESH)
        return carry

    lax.fori_loop(1, nf, greet_feat, 0)
    lax.fori_loop(nz, nz * nn, greet_node, 0)

    loads[0].wait()

    def spread(t, carry):
        for a in range(2):
            fs[a, t] = feats_v[:, pl.ds(pl.multiple_of(t * own + a * half, half), half)]
        return carry

    lax.fori_loop(0, nf, spread, 0)
    for a in range(2):
        x[a, pl.ds(pl.multiple_of(f * part, part), part), :] = fs[a, f]

    pl.semaphore_wait(barrier, nf - 1 + nz * (nn - 1))

    def feat_copy(a, to):
        return pltpu.make_async_remote_copy(
            src_ref=fs.at[a, to],
            dst_ref=x.at[a, pl.ds(pl.multiple_of(f * part, part), part)],
            send_sem=x_send.at[a],
            recv_sem=x_recv.at[a],
            device_id=(to, n),
            device_id_type=MESH,
        )

    for a in range(2):

        def send_feat(i, carry):
            feat_copy(a, lax.rem(f + i, nf)).start()
            return carry

        lax.fori_loop(1, nf, send_feat, 0)

    def all_feats(a):
        block = x.at[a, pl.ds(0, (nf - 1) * part)]
        return pltpu.make_async_remote_copy(
            src_ref=block, dst_ref=block, send_sem=x_send.at[a], recv_sem=x_recv.at[a],
            device_id=(f, n), device_id_type=MESH,
        )

    loads[1].wait()
    wt[...] = weight_v[...].T
    for k in (2, 4, 5, 6):
        loads[k].wait()
    slots = edges_v.shape[0]
    cols = 2 * nn
    count = cnt_ref[0, 0]
    for r in range(2):

        def place(c, carry):
            chosen, used = jnp.int32(0), jnp.int32(0)
            for s in range(slots):
                hit = jnp.logical_and(row_ref[0, 0, s] == r, col_ref[0, 0, s] == c)
                hit = jnp.logical_and(hit, s < count)
                chosen = chosen + jnp.where(hit, blk_ref[0, 0, s], 0)
                used = used + jnp.where(hit, 1, 0)
            block = edges_v[chosen].astype(jnp.float32)
            block = jnp.where(used > 0, block, 0.0)
            adj[c, pl.ds(r * half, half), :] = block.astype(jnp.bfloat16)
            return carry

        lax.fori_loop(0, cols, place, 0)
    loads[3].wait()

    finals = []

    def ag_len(d, a, h):
        longer = (a + h) % 2 == 0
        return 4 if longer == (d == RIGHT) else 3

    def rows_of(h):
        return pl.ds(h * hp_rows, hp_rows)

    def slot_at(d, s):
        return lax.rem(n + nn - s, nn) if d == RIGHT else lax.rem(n + s, nn)

    def to_node(d, hop):
        return lax.rem(n + hop, nn) if d == RIGHT else lax.rem(n + nn - hop, nn)

    def ag_copy(d, at, hop, a, h):
        block = p.at[slot_at(d, at), a, rows_of(h)]
        return pltpu.make_async_remote_copy(
            src_ref=block, dst_ref=block,
            send_sem=ag_send.at[d, at + hop - 1, a, h], recv_sem=ag_recv.at[d, at + hop - 1, a, h],
            device_id=(f, to_node(d, hop)), device_id_type=MESH,
        )

    def ag_pass(d, at, a, h, chosen=(4, 3, 2, 1)):
        for k in chosen:
            if AG_TREE[k] == at and k <= ag_len(d, a, h):
                copy = ag_copy(d, at, k - at, a, h)
                copy.start()
                finals.append(copy.wait_send)

    def add_block(slot, a, h, first):
        term = dot(p[slot, a, rows_of(h), :], adj[2 * slot + a], NEAR)
        if first:
            acc[rows_of(h), :] = term
        else:
            acc[rows_of(h), :] += term

    def project(a):
        all_feats(a).wait_recv()
        for w in range(2):
            rows = pl.ds(w * 128, 128)
            p[n, a, rows, :] = dot(wt[rows, :], x[a], PLAIN).astype(jnp.bfloat16)
            for h in range(w * NH // 2, (w + 1) * NH // 2):
                for d in (RIGHT, LEFT):
                    ag_pass(d, 0, a, h, (4, 3, 2))
        for h in range(NH):
            for d in (RIGHT, LEFT):
                ag_pass(d, 0, a, h, (1,))
        for h in range(NH):
            add_block(n, a, h, a == 0)

    def ag_step(k, a, h):
        got = [d for d in (RIGHT, LEFT) if k <= ag_len(d, a, h)]
        for d in got:
            block = p.at[slot_at(d, k), a, rows_of(h)]
            pltpu.make_async_remote_copy(
                src_ref=block, dst_ref=block,
                send_sem=ag_send.at[d, k - 1, a, h], recv_sem=ag_recv.at[d, k - 1, a, h],
                device_id=(f, n), device_id_type=MESH,
            ).wait_recv()
            ag_pass(d, k, a, h)

    def ag_add(k, a, h):
        for d in (RIGHT, LEFT):
            if k <= ag_len(d, a, h):
                add_block(slot_at(d, k), a, h, False)

    def activate(h):
        u = acc[rows_of(h), :]
        cdf = 0.5 * (1.0 + lax.erf(u * root_half))
        pdf = jnp.exp(-0.5 * u * u) * inv_root_two_pi
        act[rows_of(h), :] = (u * cdf).astype(jnp.bfloat16)
        grad = cot_v[rows_of(h), :].astype(jnp.float32) * (cdf + u * pdf)
        pg[rows_of(h), :] = grad.astype(jnp.bfloat16)

    def rs_len(d, h):
        return 4 if (h % 2 == 0) == (d == RIGHT) else 3

    def rs_copy(d, k, h):
        return pltpu.make_async_remote_copy(
            src_ref=rs_out.at[d, k - 1, rows_of(h)], dst_ref=rs_in.at[d, k - 1, rows_of(h)],
            send_sem=rs_send.at[d, k - 1, h], recv_sem=rs_recv.at[d, k - 1, h],
            device_id=(f, to_node(d, k - RS_TREE[k])), device_id_type=MESH,
        )

    def rs_add(total, d, k, h):
        for j in sorted(RS_TREE):
            if RS_TREE[j] == k and j <= rs_len(d, h):
                rs_copy(d, j, h).wait_recv()
                total = total + rs_in[d, j - 1, rows_of(h), :].astype(jnp.float32)
        return total

    def term(m, h):
        block = jnp.concatenate([adj[2 * m], adj[2 * m + 1]], axis=1)
        return dot(pg[rows_of(h), :], block, PLAIN)

    def rs_step(k, h):
        for d in (RIGHT, LEFT):
            if k > rs_len(d, h):
                continue
            total = rs_add(term(to_node(d, k), h), d, k, h)
            rs_out[d, k - 1, rows_of(h), :] = total.astype(jnp.bfloat16)
            copy = rs_copy(d, k, h)
            copy.start()
            finals.append(copy.wait_send)

    def rs_end(h):
        total = term(n, h)
        for d in (RIGHT, LEFT):
            total = rs_add(total, d, 0, h)
        ng[rows_of(h), :] = total.astype(jnp.bfloat16)

    def wg_copy(w, i):
        to = lax.rem(group + i, groups)
        return pltpu.make_async_remote_copy(
            src_ref=wg_out.at[w, to], dst_ref=wg_in.at[w, group],
            send_sem=wg_send.at[w], recv_sem=wg_recv.at[w],
            device_id=(feat_of(to, fz), n), device_id_type=MESH,
        )

    def wg_all(w):
        block = wg_in.at[w, pl.ds(0, groups - 1)]
        return pltpu.make_async_remote_copy(
            src_ref=block, dst_ref=block, send_sem=wg_send.at[w], recv_sem=wg_recv.at[w],
            device_id=(f, n), device_id_type=MESH,
        )

    def wg_start(w):
        units = pl.ds(w * 128, 128)
        rows = 2 * nz * part
        for q in range(groups // 2):
            features = pl.ds(q * rows, rows)
            block = dot(x[0, features, :], ng[units, pl.ds(0, half)], NEAR)
            block = block + dot(x[1, features, :], ng[units, pl.ds(half, half)], NEAR)
            block = block.astype(jnp.bfloat16).reshape(nz, 2, part, 128)
            for c in range(2):
                wg_out[w, 2 * q + c] = block[:, c]
        for i in range(1, groups):
            wg_copy(w, i).start()
        wg_in[w, group] = wg_out[w, group]

    def y_copy(i):
        z = lax.rem(fz + lax.rem(i, nz), nz)
        to = lax.rem(n + lax.div(i, nz), nn)
        return pltpu.make_async_remote_copy(
            src_ref=ys.at[z, to], dst_ref=y_in.at[fz * nn + n],
            send_sem=y_send.at[0], recv_sem=y_recv.at[0],
            device_id=(feat_of(group, z), to), device_id_type=MESH,
        )

    def y_all():
        block = y_in.at[pl.ds(0, nz * nn - 1)]
        return pltpu.make_async_remote_copy(
            src_ref=block, dst_ref=block, send_sem=y_send.at[0], recv_sem=y_recv.at[0],
            device_id=(f, n), device_id_type=MESH,
        )

    def wg_sum(w):
        wg_all(w).wait_recv()
        total = jnp.sum(wg_in[w].astype(jnp.float32), axis=0)
        for k in range(nn):
            ys[:, k, w] = total[:, 2 * k : 2 * k + 2]

    def y_exchange():
        def send_y(i, carry):
            y_copy(i).start()
            return carry

        lax.fori_loop(1, nz * nn, send_y, 0)
        y_in[fz * nn + n] = ys[fz, n]
        y_all().wait_recv()
        total = jnp.sum(y_in[...], axis=0)
        for w in range(2):
            wgrad[:, pl.ds(w * 128, 128)] = total[w]

    halves = range(NH)
    project(0)
    for k in ORDER[:2]:
        for h in halves:
            ag_step(k, 0, h)
        for h in halves:
            ag_add(k, 0, h)
    project(1)
    for h in halves:
        ag_step(ORDER[0], 1, h)
    for h in halves:
        ag_add(ORDER[0], 1, h)
    for h in halves:
        ag_step(ORDER[2], 0, h)
    for h in halves:
        ag_add(ORDER[2], 0, h)
    for h in halves:
        ag_step(ORDER[1], 1, h)
    for h in halves:
        ag_add(ORDER[1], 1, h)
    for h in halves:
        ag_step(ORDER[3], 0, h)
    for h in halves:
        ag_add(ORDER[3], 0, h)
    for h in halves:
        ag_step(ORDER[2], 1, h)
        ag_step(ORDER[3], 1, h)
        ag_add(ORDER[2], 1, h)
        ag_add(ORDER[3], 1, h)
        activate(h)
        for k in (4, 3):
            if k not in RS_TREE.values():
                rs_step(k, h)
    for k in (3, 2, 1):
        if k in RS_TREE.values() or k < 3:
            for h in halves:
                rs_step(k, h)
    for w in range(2):
        for h in range(w * NH // 2, (w + 1) * NH // 2):
            rs_end(h)
        wg_start(w)
    for w in range(2):
        wg_sum(w)
    y_exchange()
    for w in range(2):
        wg_all(w).wait_send()
    y_all().wait_send()
    for a in range(2):
        all_feats(a).wait_send()
    for wait in finals:
        wait()


def per_device(nf, nn, feats, weight, tile_row, tile_col, tile_block, tile_count, edge_blocks, cotangent):
    fin, hid = weight.shape
    own = cotangent.shape[1]
    half = own // 2
    part = feats.shape[0]
    slots = edge_blocks.shape[2]
    bf, f32 = jnp.bfloat16, jnp.float32
    vm, dma = pltpu.VMEM, pltpu.SemaphoreType.DMA
    smem = pltpu.SMEM
    anywhere = pl.BlockSpec(memory_space=pltpu.HBM)
    return pl.pallas_call(
        functools.partial(kernel, nf, nn),
        out_shape=(
            jax.ShapeDtypeStruct((hid, own), bf),
            jax.ShapeDtypeStruct((fin // (nf * nn), hid), f32),
        ),
        in_specs=[anywhere] * 3 + [pl.BlockSpec(memory_space=smem)] + [anywhere] * 4,
        out_specs=(pl.BlockSpec(memory_space=vm), pl.BlockSpec(memory_space=vm)),
        scratch_shapes=[
            smem(tile_row.shape, jnp.int32),
            smem(tile_col.shape, jnp.int32),
            smem(tile_block.shape, jnp.int32),
            vm((slots, half, half), bf),
            vm((fin, hid), bf),
            vm((hid, own), bf),
            vm(feats.shape, bf),
            vm((2, nf, part, half), bf),
            vm((hid, fin), bf),
            vm((2 * nn, own, half), bf),
            vm((2, fin, half), bf),
            vm((nn, 2, hid, half), bf),
            vm((hid, own), f32),
            vm((hid, own), bf),
            vm((2, 4, hid, own), bf),
            vm((2, 4, hid, own), bf),
            vm((hid, own), bf),
            vm((2, nf // nn, nn, part, 128), bf),
            vm((2, nf // nn, nn, part, 128), bf),
            vm((nn, nn, 2, 2, 128), f32),
            vm((nn * nn, 2, 2, 128), f32),
            dma((7,)),
            dma((2,)),
            dma((2,)),
            dma((2, 4, 2, NH)),
            dma((2, 4, 2, NH)),
            dma((2, 4, NH)),
            dma((2, 4, NH)),
            dma((2,)),
            dma((2,)),
            dma((2,)),
            dma((2,)),
        ],
        compiler_params=pltpu.CompilerParams(
            collective_id=0, has_side_effects=True, vmem_limit_bytes=40 * 1024 * 1024
        ),
        name="graphconv",
    )(*[stay(v) for v in (tile_row, tile_col, tile_block)], tile_count, *[stay(v) for v in (feats, weight, edge_blocks, cotangent)])


def stay(array):
    return pltpu.with_memory_space_constraint(array, pltpu.HBM)


def solution(mesh):
    return jax.shard_map(
        functools.partial(per_device, mesh.shape["feat"], mesh.shape["node"]),
        mesh=mesh,
        in_specs=(
            P("feat", "node"),
            P(),
            P("feat", "node", None),
            P("feat", "node", None),
            P("feat", "node", None),
            P("feat", "node"),
            P("feat", "node", None, None, None),
            P(None, ("node", "feat")),
        ),
        out_specs=(P(None, ("node", "feat")), P(("feat", "node"), None)),
        check_vma=False,
    )
```
